32 devices in a mesh: grp: 2 (over y), ctx: 4 (over z), chan: 4 (over x, core).
Axes of the slice: x: 2, y: 2, z: 4, core: 2. Of those that a mesh axis runs over, the one named last changes fastest.
Arguments:
- grad_out: bfloat16 [1024, 4096], P(('grp', 'ctx'), 'chan'), parts along dimension 0, may hold values from -6 to 6
- gate_act: bfloat16 [1024, 4096], P(('grp', 'ctx'), 'chan'), parts along dimension 0, may hold values from -6 to 6
- conv_input: bfloat16 [1024, 4096], P(('grp', 'ctx'), 'chan'), parts along dimension 0, may hold values from -0.26367188 to 0.26367188
- filter_taps: bfloat16 [512, 4096], P('ctx', 'chan'), may hold values from -0.26367188 to 0.26367188
- skip_gain: float32 [4096], P('chan'), may hold values from -4 to 4
Outputs:
- grad_input: bfloat16 [1024, 4096], P(('grp', 'ctx'), 'chan'), parts along dimension 0
- grad_filter: float32 [1024, 4096], P(('grp', 'ctx'), 'chan'), parts along dimension 0
The draws below stay inside these ranges and needn't reach their ends.
There are 2 independent parts, one for each index of `grp`. The reference program is written for one: setup_inputs(seed, part) draws one part's arguments, and reference() takes and returns one part's arrays. A program takes and returns all parts, laid end to end along the dimension named above; an argument that names none is the same for every part. Nothing has to cross between parts.
All inputs are finite; a program needn't handle non-finite values.
Results may differ from the reference program's by a relative error of at most 0.014.
Values may be sent and summed in bfloat16 or wider, within the bound.
No kernel may reach another device: no remote copies, remote signals or barrier semaphores. Data moves between devices by JAX's collectives and lax.ppermute only.
A program may use at most 64 MiB of HBM per device.

```python
import jax
import jax.numpy as jnp
from jax import lax

D = 4096
SEQ = 512


def steps_of(stream_key, dims, shards, smallest, largest):
    level = 1.0
    for axis_at, parts in shards:
        steps = jax.random.uniform(jax.random.fold_in(jax.random.fold_in(stream_key, 6), axis_at), (parts,), jnp.float32, smallest / len(shards), largest / len(shards))
        level = level * jnp.repeat(jnp.exp(steps), dims[axis_at] // parts).reshape((-1,) + (1,) * (len(dims) - 1 - axis_at))
    return level


def centred(own_key, dims, deviation, reach, cuts=(), dtype=jnp.bfloat16):
    factor_of = steps_of(own_key, dims, cuts, -0.22, 0.18) if cuts else 1.0
    values = jax.random.normal(own_key, dims, jnp.float32) * deviation * factor_of
    return jnp.minimum(jnp.maximum(values, -reach), reach).astype(dtype)


def setup_inputs(seed: int = 0, part: int = 0) -> dict:
    arg_keys = jax.random.split(jax.random.key(seed), 6)
    part_keys = jax.random.split(jax.random.fold_in(arg_keys[5], part), 6)
    return {
        "grad_out": centred(part_keys[0], (SEQ, D), 1.0, 6.0, ((0, 4), (1, 4))),
        "gate_act": centred(part_keys[1], (SEQ, D), 1.0, 6.0, ((0, 4), (1, 4))),
        "conv_input": centred(part_keys[2], (SEQ, D), (1.0 / SEQ ** 0.5), 0.26367188, ((0, 4), (1, 4))),
        "filter_taps": centred(arg_keys[3], (SEQ, D), (1.0 / SEQ ** 0.5), 0.26367188, ((0, 4), (1, 4))),
        "skip_gain": centred(arg_keys[4], (D,), 1.0, 4.0, ((0, 4),), jnp.float32),
    }


def reference(grad_out, gate_act, conv_input, filter_taps, skip_gain):
    grad_y = (grad_out.astype(jnp.float32) * gate_act.astype(jnp.float32)).astype(jnp.bfloat16)
    grad_y = lax.optimization_barrier(grad_y).astype(jnp.float32)
    length = 2 * SEQ
    grad_freq = jnp.fft.rfft(grad_y, n=length, axis=0)
    taps_freq = jnp.fft.rfft(filter_taps.astype(jnp.float32), n=length, axis=0)
    input_freq = jnp.fft.rfft(conv_input.astype(jnp.float32), n=length, axis=0)
    conv_part = jnp.fft.irfft(grad_freq * jnp.conj(taps_freq), n=length, axis=0)[:SEQ]
    grad_filter = jnp.fft.irfft(grad_freq * jnp.conj(input_freq), n=length, axis=0)[:SEQ]
    grad_input = (conv_part + skip_gain.astype(jnp.float32)[None, :] * grad_y).astype(jnp.bfloat16)
    return grad_input, grad_filter.astype(jnp.float32)
```

```python
import functools

import jax
import jax.numpy as jnp
import ml_dtypes
import numpy as np
from jax import lax
from jax.sharding import PartitionSpec as P


@functools.cache
def tables(seq):
    bins = np.arange(seq)[:, None] * 2 + 1
    places = np.arange(seq)[None, :]
    angles = (bins * places % (4 * seq)) * (np.pi / (2 * seq))
    forward = np.concatenate([np.cos(angles), np.sin(angles)], axis=0)
    inverse = np.concatenate([np.cos(angles), np.sin(angles)], axis=0).T / seq
    return forward.astype(ml_dtypes.bfloat16), inverse.astype(ml_dtypes.bfloat16)


def shards(grad_out, gate_act, conv_input, filter_taps, skip_gain):
    span, channels = grad_out.shape
    parts = lax.axis_size("ctx")
    own = lax.axis_index("ctx")
    seq = span * parts
    width = channels // parts
    forward, inverse = tables(seq)
    shifts = sorted(range(1, parts), key=lambda s: (abs(2 * s - parts), s))

    def moved(piece, shift):
        return lax.ppermute(piece, "ctx", [(i, (i + shift) % parts) for i in range(parts)])

    def scatter(values):
        pieces = [None] * parts
        pieces[0] = lax.dynamic_slice_in_dim(values, own * width, width, 1)
        for shift in shifts:
            target = (own + shift) % parts
            pieces[parts - shift] = moved(
                lax.dynamic_slice_in_dim(values, target * width, width, 1), shift
            )
        ahead = jnp.concatenate(pieces + pieces, axis=0)
        return lax.dynamic_slice_in_dim(ahead, (parts - own) % parts * span, seq, 0)

    def gather(values):
        pieces = [None] * parts
        pieces[0] = lax.dynamic_slice_in_dim(values, own * span, span, 0)
        for shift in shifts:
            target = (own + shift) % parts
            pieces[parts - shift] = moved(
                lax.dynamic_slice_in_dim(values, target * span, span, 0), shift
            )
        ahead = jnp.concatenate(pieces + pieces, axis=1)
        return lax.dynamic_slice_in_dim(ahead, (parts - own) % parts * width, channels, 1)

    def spectrum(signal):
        both = jnp.dot(forward, signal, preferred_element_type=jnp.float32)
        return both[:seq], both[seq:]

    def correlate(first, second):
        real = first[0] * second[0] + first[1] * second[1]
        imag = first[1] * second[0] - first[0] * second[1]
        both = jnp.concatenate([real, imag], axis=0).astype(jnp.bfloat16)
        return jnp.dot(inverse, both, preferred_element_type=jnp.float32)

    grad_y = (grad_out.astype(jnp.float32) * gate_act.astype(jnp.float32)).astype(jnp.bfloat16)
    taps = scatter(filter_taps)
    grads = scatter(grad_y)
    inputs = scatter(conv_input)
    gain = lax.dynamic_slice_in_dim(skip_gain, own * width, width, 0)
    grad_spec = spectrum(grads)
    conv_part = correlate(grad_spec, spectrum(taps))
    grad_input = (conv_part + gain[None, :] * grads.astype(jnp.float32)).astype(jnp.bfloat16)
    grad_input = gather(grad_input)
    grad_filter = gather(correlate(grad_spec, spectrum(inputs)).astype(jnp.bfloat16))
    return grad_input, grad_filter.astype(jnp.float32)


def solution(mesh):
    return jax.shard_map(
        shards,
        mesh=mesh,
        in_specs=(
            P(("grp", "ctx"), "chan"),
            P(("grp", "ctx"), "chan"),
            P(("grp", "ctx"), "chan"),
            P("ctx", "chan"),
            P("chan"),
        ),
        out_specs=(P(("grp", "ctx"), "chan"), P(("grp", "ctx"), "chan")),
        check_vma=False,
    )
```

```python
import functools

import jax
import jax.numpy as jnp
import ml_dtypes
import numpy as np
from jax import lax
from jax.experimental import pallas as pl
from jax.experimental.pallas import tpu as pltpu
from jax.sharding import PartitionSpec as P

KIB = 1 << 10
CHUNKS = 8
ORDER = (1, 2, 3)


@functools.cache
def tables(seq):
    bins = np.arange(seq)[:, None] * 2 + 1
    places = np.arange(seq)[None, :]
    angles = (bins * places % (4 * seq)) * (np.pi / (2 * seq))
    return np.concatenate([np.cos(angles), np.sin(angles)]).astype(ml_dtypes.bfloat16)


def rows(count, width, dtype=jnp.bfloat16):
    return jax.ShapeDtypeStruct((count, width), dtype)


def call(body, outs, args, flops, scratch=(), limit=8192 * KIB, space=pltpu.VMEM):
    size = sum(a.size * a.dtype.itemsize for a in (*outs, *args))
    return pl.pallas_call(
        body,
        out_shape=outs,
        in_specs=[pl.BlockSpec(memory_space=space)] * len(args),
        out_specs=[pl.BlockSpec(memory_space=pltpu.VMEM)] * len(outs),
        scratch_shapes=list(scratch),
        compiler_params=pltpu.CompilerParams(vmem_limit_bytes=limit),
        cost_estimate=pl.CostEstimate(flops=flops, bytes_accessed=size, transcendentals=0),
    )(*args)


def part(index, size):
    return pl.ds(pl.multiple_of(index * size, size), size)


def behind(own, shift, parts):
    return lax.rem(own - shift + parts, parts)


def ahead(own, shift, parts):
    return lax.rem(own + shift, parts)


def split_body(parts, *refs):
    sources, pieces, (held, sems) = refs[:4], refs[4:-2], refs[-2:]
    copies = [pltpu.make_async_copy(source, held.at[n], sems.at[n]) for n, source in enumerate(sources)]
    for copy in copies:
        copy.start()
    outer, gate, inputs, taps = (held.at[n] for n in range(4))
    own = lax.axis_index("ctx")
    width = outer.shape[1] // parts
    for copy in copies:
        copy.wait()
    for shift in range(parts):
        lanes = part(ahead(own, shift, parts), width)
        pieces[shift][...] = taps[:, lanes]
        product = outer[:, lanes].astype(jnp.float32) * gate[:, lanes].astype(jnp.float32)
        pieces[parts + shift][...] = product.astype(jnp.bfloat16)
        pieces[2 * parts + shift][...] = inputs[:, lanes]


def load_body(table, gain, anchor, table_out, gain_out, sems):
    size = table.shape[0] // CHUNKS
    copies = [(table.at[pl.ds(n * size, size)], table_out.at[pl.ds(n * size, size)]) for n in range(CHUNKS)]
    copies = [pltpu.make_async_copy(*ends, sems.at[n]) for n, ends in enumerate(copies + [(gain, gain_out)])]
    for copy in copies:
        copy.start()
    for copy in copies:
        copy.wait()


def dot(first, second):
    return jnp.dot(first, second, preferred_element_type=jnp.float32)


def stack(pieces, out):
    own, parts, span = lax.axis_index("ctx"), len(pieces), pieces[0].shape[0]
    for shift, piece in enumerate(pieces):
        out[part(behind(own, shift, parts), span), :] = piece[...]


def correlate(first, second, table, both):
    seq = both.shape[0] // 2
    real, imag = first[:seq], first[seq:]
    cos, sin = second[:seq], second[seq:]
    both[:seq, :] = (real * cos + imag * sin).astype(jnp.bfloat16)
    both[seq:, :] = (imag * cos - real * sin).astype(jnp.bfloat16)
    product = lax.dot_general(table[...], both[...], (((0,), (0,)), ((), ())), preferred_element_type=jnp.float32)
    return product * (1.0 / seq)


def emit(outs, total):
    own, parts, span = lax.axis_index("ctx"), len(outs), outs[0].shape[0]
    for shift, out in enumerate(outs):
        out[...] = total[part(ahead(own, shift, parts), span), :].astype(jnp.bfloat16)


def input_body(parts, gain, *refs):
    tap_pieces, grad_pieces, refs = refs[:parts], refs[parts : 2 * parts], refs[2 * parts :]
    table, spec, refs = refs[0], refs[1], refs[2:]
    outs, (taps, grads, both, total) = refs[:parts], refs[parts:]
    stack(tap_pieces, taps)
    stack(grad_pieces, grads)
    grad_spec = dot(table[...], grads[...])
    spec[...] = grad_spec
    skip = gain[:, part(lax.axis_index("ctx"), taps.shape[1])] * grads[...].astype(jnp.float32)
    total[...] = correlate(grad_spec, dot(table[...], taps[...]), table, both) + skip
    emit(outs, total)


def filter_body(parts, spec, *refs):
    pieces, table, refs = refs[:parts], refs[parts], refs[parts + 1 :]
    outs, (inputs, both, total) = refs[:parts], refs[parts:]
    stack(pieces, inputs)
    total[...] = correlate(spec, dot(table[...], inputs[...]), table, both)
    emit(outs, total)


def join_body(*refs):
    pieces, out = refs[:-1], refs[-1]
    own, parts, width = lax.axis_index("ctx"), len(pieces), pieces[0].shape[1]
    for shift, piece in enumerate(pieces):
        out[:, part(behind(own, shift, parts), width)] = piece[...].astype(out.dtype)


def plain_shards(grad_out, gate_act, conv_input, filter_taps, skip_gain):
    span, channels = grad_out.shape
    parts = lax.axis_size("ctx")
    own = lax.axis_index("ctx")
    seq = span * parts
    width = channels // parts
    table = jnp.asarray(tables(seq))

    def swap(values, size, axis, place, other):
        pieces = [None] * parts
        for shift in range(parts):
            piece = lax.dynamic_slice_in_dim(values, (own + shift) % parts * size, size, axis)
            pairs = [(i, (i + shift) % parts) for i in range(parts)]
            pieces[-shift % parts] = lax.ppermute(piece, "ctx", pairs) if shift else piece
        ring = jnp.concatenate(pieces + pieces, axis=other)
        start = (parts - own) % parts * place
        return lax.dynamic_slice_in_dim(ring, start, parts * place, other)

    def correlate(first, second):
        real, imag = first[:seq], first[seq:]
        cos, sin = second[:seq], second[seq:]
        both = jnp.concatenate([real * cos + imag * sin, imag * cos - real * sin], axis=0).astype(jnp.bfloat16)
        return lax.dot_general(table, both, (((0,), (0,)), ((), ())), preferred_element_type=jnp.float32) * (1.0 / seq)

    grad_y = (grad_out.astype(jnp.float32) * gate_act.astype(jnp.float32)).astype(jnp.bfloat16)
    taps, grads, inputs = (swap(v, width, 1, span, 0) for v in (filter_taps, grad_y, conv_input))
    gain = lax.dynamic_slice_in_dim(skip_gain, own * width, width, 0)
    spec = dot(table, grads)
    grad_input = correlate(spec, dot(table, taps)) + gain[None, :] * grads.astype(jnp.float32)
    grad_filter = correlate(spec, dot(table, inputs))
    grad_input, grad_filter = (swap(v.astype(jnp.bfloat16), span, 0, width, 1) for v in (grad_input, grad_filter))
    return grad_input, grad_filter.astype(jnp.float32)


def shards(grad_out, gate_act, conv_input, filter_taps, skip_gain):
    span, channels = grad_out.shape
    parts = lax.axis_size("ctx")
    seq = span * parts
    width = channels // parts
    if width % 128 or span % 16 or parts != 4:
        return plain_shards(grad_out, gate_act, conv_input, filter_taps, skip_gain)

    def moved(pieces, shifts=ORDER):
        pieces = list(pieces)
        for shift in shifts:
            pieces[shift] = lax.ppermute(pieces[shift], "ctx", [(i, (i + shift) % parts) for i in range(parts)])
        return pieces

    small, bf16, f32 = rows(span, width), jnp.bfloat16, jnp.float32
    split = call(
        functools.partial(split_body, parts),
        [small] * (3 * parts),
        (grad_out, gate_act, conv_input, filter_taps),
        span * channels,
        (pltpu.VMEM((4, span, channels), bf16), pltpu.SemaphoreType.DMA((4,))),
        limit=54336 * KIB,
        space=pltpu.HBM,
    )
    taps = moved(split[:parts])
    grads = moved(split[parts : 2 * parts])
    inputs = list(split[2 * parts : 3 * parts])

    inputs = moved(inputs, ORDER)
    table, gain = call(
        load_body,
        [rows(2 * seq, seq), rows(1, channels, f32)],
        (jnp.asarray(tables(seq)), skip_gain[None, :], taps[ORDER[0]]),
        0,
        (pltpu.SemaphoreType.DMA((CHUNKS + 1,)),),
        limit=53312 * KIB,
        space=pltpu.HBM,
    )
    series, spectra, total = pltpu.VMEM((seq, width), bf16), pltpu.VMEM((2 * seq, width), bf16), pltpu.VMEM((seq, width), f32)
    spec, *grad_inputs = call(
        functools.partial(input_body, parts),
        [rows(2 * seq, width, f32)] + [small] * parts,
        (gain, *taps, *grads, table),
        12 * seq * seq * width,
        (series, series, spectra, total),
    )

    grad_inputs = moved(grad_inputs)
    grad_filters = call(
        functools.partial(filter_body, parts),
        [small] * parts,
        (spec, *inputs, table),
        8 * seq * seq * width,
        (series, spectra, total),
    )
    grad_filters = moved(grad_filters)
    grad_input = call(join_body, [rows(span, channels)], grad_inputs, 0)[0]
    grad_filter = call(join_body, [rows(span, channels, f32)], grad_filters, 0)[0]
    return grad_input, grad_filter


def solution(mesh):
    return jax.shard_map(
        shards,
        mesh=mesh,
        in_specs=(
            P(("grp", "ctx"), "chan"),
            P(("grp", "ctx"), "chan"),
            P(("grp", "ctx"), "chan"),
            P("ctx", "chan"),
            P("chan"),
        ),
        out_specs=(P(("grp", "ctx"), "chan"), P(("grp", "ctx"), "chan")),
        check_vma=False,
    )
```

```python
import functools

import jax
import jax.numpy as jnp
import ml_dtypes
import numpy as np
from jax import lax
from jax.experimental import pallas as pl
from jax.experimental.pallas import tpu as pltpu
from jax.sharding import PartitionSpec as P

KIB = 1 << 10
CHUNKS = 8
PIECES = 2
H, G, U, I, F = ((0,2,3,1),(0,1,2,3),(0,1,2,3),(0,1,2,3),(0,1,2,3))


@functools.cache
def tables(seq):
    bins = np.arange(seq)[:, None] * 2 + 1
    places = np.arange(seq)[None, :]
    angles = (bins * places % (4 * seq)) * (np.pi / (2 * seq))
    return np.concatenate([np.cos(angles), np.sin(angles)]).astype(ml_dtypes.bfloat16)


def rows(count, width, dtype=jnp.bfloat16):
    return jax.ShapeDtypeStruct((count, width), dtype)


def call(body, outs, args, flops, scratch=(), limit=8192 * KIB, space=pltpu.VMEM):
    size = sum(a.size * a.dtype.itemsize for a in (*outs, *args))
    return pl.pallas_call(
        body,
        out_shape=outs,
        in_specs=[pl.BlockSpec(memory_space=space)] * len(args),
        out_specs=[pl.BlockSpec(memory_space=pltpu.VMEM)] * len(outs),
        scratch_shapes=list(scratch),
        compiler_params=pltpu.CompilerParams(vmem_limit_bytes=limit),
        cost_estimate=pl.CostEstimate(flops=flops, bytes_accessed=size, transcendentals=0),
    )(*args)


def part(index, size):
    return pl.ds(pl.multiple_of(index * size, size), size)


def behind(own, shift, parts):
    return lax.rem(own - shift + parts, parts)


def ahead(own, shift, parts):
    return lax.rem(own + shift, parts)


def split_body(parts, *refs):
    sources, pieces, (held, sems) = refs[:4], refs[4:-2], refs[-2:]
    copies = [pltpu.make_async_copy(source, held.at[n], sems.at[n]) for n, source in enumerate(sources)]
    for copy in copies:
        copy.start()
    outer, gate, inputs, taps = (held.at[n] for n in range(4))
    own = lax.axis_index("ctx")
    width = outer.shape[1] // parts
    for copy in copies:
        copy.wait()
    for shift in range(parts):
        lanes = part(ahead(own, shift, parts), width)
        pieces[shift][...] = taps[:, lanes]
        product = outer[:, lanes].astype(jnp.float32) * gate[:, lanes].astype(jnp.float32)
        pieces[parts + shift][...] = product.astype(jnp.bfloat16)
        pieces[2 * parts + shift][...] = inputs[:, lanes]


def load_body(table, gain, anchor, table_out, gain_out, sems):
    size = table.shape[0] // CHUNKS
    copies = [(table.at[pl.ds(n * size, size)], table_out.at[pl.ds(n * size, size)]) for n in range(CHUNKS)]
    copies = [pltpu.make_async_copy(*ends, sems.at[n]) for n, ends in enumerate(copies + [(gain, gain_out)])]
    for copy in copies:
        copy.start()
    for copy in copies:
        copy.wait()


def dot(first, second):
    return jnp.dot(first, second, preferred_element_type=jnp.float32)


def stack(pieces, out, order):
    own, parts, span = lax.axis_index("ctx"), len(pieces), pieces[0].shape[0]
    for shift, piece in zip(order, pieces):
        out[part(behind(own, shift, parts), span), :] = piece[...]


def correlate(grads, seconds, table, spec, fresh):
    seq = grads.shape[0] if fresh else seconds.shape[0]
    size = seq // PIECES
    total = None
    for n in range(PIECES):
        cos_rows, sin_rows = slice(n * size, (n + 1) * size), slice(seq + n * size, seq + (n + 1) * size)
        if fresh:
            real, imag = dot(table[cos_rows, :], grads[...]), dot(table[sin_rows, :], grads[...])
            spec[cos_rows, :], spec[sin_rows, :] = real, imag
        else:
            real, imag = spec[cos_rows, :], spec[sin_rows, :]
        cos, sin = dot(table[cos_rows, :], seconds[...]), dot(table[sin_rows, :], seconds[...])
        both = (real * cos + imag * sin).astype(jnp.bfloat16), (imag * cos - real * sin).astype(jnp.bfloat16)
        for rows_at, values in zip((cos_rows, sin_rows), both):
            term = lax.dot_general(table[rows_at, :], values, (((0,), (0,)), ((), ())), preferred_element_type=jnp.float32)
            total = term if total is None else total + term
    return total * (1.0 / seq)


def emit(outs, total):
    own, parts, span = lax.axis_index("ctx"), len(outs), outs[0].shape[0]
    for shift, out in enumerate(outs):
        out[...] = total[part(ahead(own, shift, parts), span), :].astype(jnp.bfloat16)


def input_body(parts, gain, *refs):
    tap_pieces, grad_pieces, refs = refs[:parts], refs[parts : 2 * parts], refs[2 * parts :]
    table, spec, refs = refs[0], refs[1], refs[2:]
    outs, (taps, grads, both, total) = refs[:parts], refs[parts:]
    stack(tap_pieces, taps, H)
    stack(grad_pieces, grads, G)
    skip = gain[:, part(lax.axis_index("ctx"), taps.shape[1])] * grads[...].astype(jnp.float32)
    total[...] = correlate(grads, taps, table, spec, True) + skip
    emit(outs, total)


def filter_body(parts, spec, *refs):
    pieces, table, refs = refs[:parts], refs[parts], refs[parts + 1 :]
    outs, (inputs, both, total) = refs[:parts], refs[parts:]
    stack(pieces, inputs, U)
    total[...] = correlate(None, inputs, table, spec, False)
    emit(outs, total)


def join_body(order, *refs):
    pieces, out = refs[:-1], refs[-1]
    own, parts, width = lax.axis_index("ctx"), len(pieces), pieces[0].shape[1]
    for shift, piece in zip(order, pieces):
        out[:, part(behind(own, shift, parts), width)] = piece[...].astype(out.dtype)


def plain_shards(grad_out, gate_act, conv_input, filter_taps, skip_gain):
    span, channels = grad_out.shape
    parts = lax.axis_size("ctx")
    own = lax.axis_index("ctx")
    seq = span * parts
    width = channels // parts
    table = jnp.asarray(tables(seq))

    def swap(values, size, axis, place, other):
        pieces = [None] * parts
        for shift in range(parts):
            piece = lax.dynamic_slice_in_dim(values, (own + shift) % parts * size, size, axis)
            pairs = [(i, (i + shift) % parts) for i in range(parts)]
            pieces[-shift % parts] = lax.ppermute(piece, "ctx", pairs) if shift else piece
        ring = jnp.concatenate(pieces + pieces, axis=other)
        start = (parts - own) % parts * place
        return lax.dynamic_slice_in_dim(ring, start, parts * place, other)

    def correlate(first, second):
        real, imag = first[:seq], first[seq:]
        cos, sin = second[:seq], second[seq:]
        both = jnp.concatenate([real * cos + imag * sin, imag * cos - real * sin], axis=0).astype(jnp.bfloat16)
        return lax.dot_general(table, both, (((0,), (0,)), ((), ())), preferred_element_type=jnp.float32) * (1.0 / seq)

    grad_y = (grad_out.astype(jnp.float32) * gate_act.astype(jnp.float32)).astype(jnp.bfloat16)
    taps, grads, inputs = (swap(v, width, 1, span, 0) for v in (filter_taps, grad_y, conv_input))
    gain = lax.dynamic_slice_in_dim(skip_gain, own * width, width, 0)
    spec = dot(table, grads)
    grad_input = correlate(spec, dot(table, taps)) + gain[None, :] * grads.astype(jnp.float32)
    grad_filter = correlate(spec, dot(table, inputs))
    grad_input, grad_filter = (swap(v.astype(jnp.bfloat16), span, 0, width, 1) for v in (grad_input, grad_filter))
    return grad_input, grad_filter.astype(jnp.float32)


def shards(grad_out, gate_act, conv_input, filter_taps, skip_gain):
    span, channels = grad_out.shape
    parts = lax.axis_size("ctx")
    seq = span * parts
    width = channels // parts
    if width % 128 or span % 16 or parts != 4:
        return plain_shards(grad_out, gate_act, conv_input, filter_taps, skip_gain)

    def moved(pieces, order):
        pairs = [[(i, (i + shift) % parts) for i in range(parts)] for shift in order]
        return [lax.ppermute(pieces[n], "ctx", pair) if n else pieces[n] for n, pair in zip(order, pairs)]

    small, bf16, f32 = rows(span, width), jnp.bfloat16, jnp.float32
    split = call(
        functools.partial(split_body, parts),
        [small] * (3 * parts),
        (grad_out, gate_act, conv_input, filter_taps),
        span * channels,
        (pltpu.VMEM((4, span, channels), bf16), pltpu.SemaphoreType.DMA((4,))),
        limit=54336 * KIB,
        space=pltpu.HBM,
    )
    taps = moved(split[:parts], H)
    grads = moved(split[parts : 2 * parts], G)
    inputs = moved(split[2 * parts :], U)
    table, gain = call(
        load_body,
        [rows(2 * seq, seq), rows(1, channels, f32)],
        (jnp.asarray(tables(seq)), skip_gain[None, :], taps[1]),
        0,
        (pltpu.SemaphoreType.DMA((CHUNKS + 1,)),),
        limit=53312 * KIB,
        space=pltpu.HBM,
    )
    series, spectra, total = pltpu.VMEM((seq, width), bf16), pltpu.VMEM((2 * seq, width), bf16), pltpu.VMEM((seq, width), f32)
    spec, *grad_inputs = call(
        functools.partial(input_body, parts),
        [rows(2 * seq, width, f32)] + [small] * parts,
        (gain, *taps, *grads, table),
        12 * seq * seq * width,
        (series, series, spectra, total),
    )
    grad_inputs = moved(grad_inputs, I)
    grad_filters = call(
        functools.partial(filter_body, parts),
        [small] * parts,
        (spec, *inputs, table),
        8 * seq * seq * width,
        (series, spectra, total),
    )
    grad_filters = moved(grad_filters, F)
    grad_input = call(functools.partial(join_body, I), [rows(span, channels)], grad_inputs, 0)[0]
    grad_filter = call(functools.partial(join_body, F), [rows(span, channels, f32)], grad_filters, 0)[0]
    return grad_input, grad_filter


def solution(mesh):
    return jax.shard_map(
        shards,
        mesh=mesh,
        in_specs=(
            P(("grp", "ctx"), "chan"),
            P(("grp", "ctx"), "chan"),
            P(("grp", "ctx"), "chan"),
            P("ctx", "chan"),
            P("chan"),
        ),
        out_specs=(P(("grp", "ctx"), "chan"), P(("grp", "ctx"), "chan")),
        check_vma=False,
    )
```

```python
import functools

import jax
import jax.numpy as jnp
import ml_dtypes
import numpy as np
from jax import lax
from jax.experimental import pallas as pl
from jax.experimental.pallas import tpu as pltpu
from jax.sharding import PartitionSpec as P

KIB = 1 << 10
CHUNKS = 8
PIECES = 2
H, G, U, I, F = ((0,2,3,1),(0,1,2,3),(0,1,2,3),(0,1,2,3),(0,1,2,3))


@functools.cache
def tables(seq):
    bins = np.arange(seq)[:, None] * 2 + 1
    places = np.arange(seq)[None, :]
    angles = (bins * places % (4 * seq)) * (np.pi / (2 * seq))
    return np.concatenate([np.cos(angles), np.sin(angles)]).astype(ml_dtypes.bfloat16)


def rows(count, width, dtype=jnp.bfloat16):
    return jax.ShapeDtypeStruct((count, width), dtype)


def call(body, outs, args, flops, scratch=(), limit=8192 * KIB, space=pltpu.VMEM):
    size = sum(a.size * a.dtype.itemsize for a in (*outs, *args))
    return pl.pallas_call(
        body,
        out_shape=outs,
        in_specs=[pl.BlockSpec(memory_space=space)] * len(args),
        out_specs=[pl.BlockSpec(memory_space=pltpu.VMEM)] * len(outs),
        scratch_shapes=list(scratch),
        compiler_params=pltpu.CompilerParams(vmem_limit_bytes=limit),
        cost_estimate=pl.CostEstimate(flops=flops, bytes_accessed=size, transcendentals=0),
    )(*args)


def part(index, size):
    return pl.ds(pl.multiple_of(index * size, size), size)


def behind(own, shift, parts):
    return lax.rem(own - shift + parts, parts)


def ahead(own, shift, parts):
    return lax.rem(own + shift, parts)


def split_body(parts, *refs):
    sources, pieces, (held, sems) = refs[:4], refs[4:-2], refs[-2:]
    copies = [pltpu.make_async_copy(source, held.at[n], sems.at[n]) for n, source in enumerate(sources)]
    for copy in copies[::-1]:
        copy.start()
    outer, gate, inputs, taps = (held.at[n] for n in range(4))
    own = lax.axis_index("ctx")
    width = outer.shape[1] // parts
    copies[3].wait()
    for shift in range(parts):
        pieces[shift][...] = taps[:, part(ahead(own, shift, parts), width)]
    copies[2].wait()
    for shift in range(parts):
        pieces[2 * parts + shift][...] = inputs[:, part(ahead(own, shift, parts), width)]
    copies[0].wait()
    copies[1].wait()
    for shift in range(parts):
        lanes = part(ahead(own, shift, parts), width)
        product = outer[:, lanes].astype(jnp.float32) * gate[:, lanes].astype(jnp.float32)
        pieces[parts + shift][...] = product.astype(jnp.bfloat16)


def load_body(table, gain, anchor, table_out, gain_out, sems):
    size = table.shape[0] // CHUNKS
    copies = [(table.at[pl.ds(n * size, size)], table_out.at[pl.ds(n * size, size)]) for n in range(CHUNKS)]
    copies = [pltpu.make_async_copy(*ends, sems.at[n]) for n, ends in enumerate(copies + [(gain, gain_out)])]
    for copy in copies:
        copy.start()
    for copy in copies:
        copy.wait()


def dot(first, second):
    return jnp.dot(first, second, preferred_element_type=jnp.float32)


def stack(pieces, out, order):
    own, parts, span = lax.axis_index("ctx"), len(pieces), pieces[0].shape[0]
    for shift, piece in zip(order, pieces):
        out[part(behind(own, shift, parts), span), :] = piece[...]


def correlate(grads, seconds, table, spec, fresh):
    seq = grads.shape[0] if fresh else seconds.shape[0]
    size = seq // PIECES
    total = None
    for n in range(PIECES):
        cos_rows, sin_rows = slice(n * size, (n + 1) * size), slice(seq + n * size, seq + (n + 1) * size)
        if fresh:
            real, imag = dot(table[cos_rows, :], grads[...]), dot(table[sin_rows, :], grads[...])
            spec[cos_rows, :], spec[sin_rows, :] = real, imag
        else:
            real, imag = spec[cos_rows, :], spec[sin_rows, :]
        cos, sin = dot(table[cos_rows, :], seconds[...]), dot(table[sin_rows, :], seconds[...])
        both = (real * cos + imag * sin).astype(jnp.bfloat16), (imag * cos - real * sin).astype(jnp.bfloat16)
        for rows_at, values in zip((cos_rows, sin_rows), both):
            term = lax.dot_general(table[rows_at, :], values, (((0,), (0,)), ((), ())), preferred_element_type=jnp.float32)
            total = term if total is None else total + term
    return total * (1.0 / seq)


def emit(outs, total):
    own, parts, span = lax.axis_index("ctx"), len(outs), outs[0].shape[0]
    for shift, out in enumerate(outs):
        out[...] = total[part(ahead(own, shift, parts), span), :].astype(jnp.bfloat16)


def input_body(parts, gain, *refs):
    tap_pieces, grad_pieces, refs = refs[:parts], refs[parts : 2 * parts], refs[2 * parts :]
    table, spec, refs = refs[0], refs[1], refs[2:]
    outs, (taps, grads, both, total) = refs[:parts], refs[parts:]
    stack(tap_pieces, taps, H)
    stack(grad_pieces, grads, G)
    skip = gain[:, part(lax.axis_index("ctx"), taps.shape[1])] * grads[...].astype(jnp.float32)
    total[...] = correlate(grads, taps, table, spec, True) + skip
    emit(outs, total)


def filter_body(parts, spec, *refs):
    pieces, table, refs = refs[:parts], refs[parts], refs[parts + 1 :]
    outs, (inputs, both, total) = refs[:parts], refs[parts:]
    stack(pieces, inputs, U)
    total[...] = correlate(None, inputs, table, spec, False)
    emit(outs, total)


def join_body(order, *refs):
    pieces, out = refs[:-1], refs[-1]
    own, parts, width = lax.axis_index("ctx"), len(pieces), pieces[0].shape[1]
    for shift, piece in zip(order, pieces):
        out[:, part(behind(own, shift, parts), width)] = piece[...].astype(out.dtype)


def plain_shards(grad_out, gate_act, conv_input, filter_taps, skip_gain):
    span, channels = grad_out.shape
    parts = lax.axis_size("ctx")
    own = lax.axis_index("ctx")
    seq = span * parts
    width = channels // parts
    table = jnp.asarray(tables(seq))

    def swap(values, size, axis, place, other):
        pieces = [None] * parts
        for shift in range(parts):
            piece = lax.dynamic_slice_in_dim(values, (own + shift) % parts * size, size, axis)
            pairs = [(i, (i + shift) % parts) for i in range(parts)]
            pieces[-shift % parts] = lax.ppermute(piece, "ctx", pairs) if shift else piece
        ring = jnp.concatenate(pieces + pieces, axis=other)
        start = (parts - own) % parts * place
        return lax.dynamic_slice_in_dim(ring, start, parts * place, other)

    def correlate(first, second):
        real, imag = first[:seq], first[seq:]
        cos, sin = second[:seq], second[seq:]
        both = jnp.concatenate([real * cos + imag * sin, imag * cos - real * sin], axis=0).astype(jnp.bfloat16)
        return lax.dot_general(table, both, (((0,), (0,)), ((), ())), preferred_element_type=jnp.float32) * (1.0 / seq)

    grad_y = (grad_out.astype(jnp.float32) * gate_act.astype(jnp.float32)).astype(jnp.bfloat16)
    taps, grads, inputs = (swap(v, width, 1, span, 0) for v in (filter_taps, grad_y, conv_input))
    gain = lax.dynamic_slice_in_dim(skip_gain, own * width, width, 0)
    spec = dot(table, grads)
    grad_input = correlate(spec, dot(table, taps)) + gain[None, :] * grads.astype(jnp.float32)
    grad_filter = correlate(spec, dot(table, inputs))
    grad_input, grad_filter = (swap(v.astype(jnp.bfloat16), span, 0, width, 1) for v in (grad_input, grad_filter))
    return grad_input, grad_filter.astype(jnp.float32)


def shards(grad_out, gate_act, conv_input, filter_taps, skip_gain):
    span, channels = grad_out.shape
    parts = lax.axis_size("ctx")
    seq = span * parts
    width = channels // parts
    if width % 128 or span % 16 or parts != 4:
        return plain_shards(grad_out, gate_act, conv_input, filter_taps, skip_gain)

    def moved(pieces, order):
        pairs = [[(i, (i + shift) % parts) for i in range(parts)] for shift in order]
        return [lax.ppermute(pieces[n], "ctx", pair) if n else pieces[n] for n, pair in zip(order, pairs)]

    small, bf16, f32 = rows(span, width), jnp.bfloat16, jnp.float32
    split = call(
        functools.partial(split_body, parts),
        [small] * (3 * parts),
        (grad_out, gate_act, conv_input, filter_taps),
        span * channels,
        (pltpu.VMEM((4, span, channels), bf16), pltpu.SemaphoreType.DMA((4,))),
        limit=54336 * KIB,
        space=pltpu.HBM,
    )
    taps = moved(split[:parts], H)
    grads = moved(split[parts : 2 * parts], G)
    inputs = moved(split[2 * parts :], U)
    table, gain = call(
        load_body,
        [rows(2 * seq, seq), rows(1, channels, f32)],
        (jnp.asarray(tables(seq)), skip_gain[None, :], taps[1]),
        0,
        (pltpu.SemaphoreType.DMA((CHUNKS + 1,)),),
        limit=53312 * KIB,
        space=pltpu.HBM,
    )
    series, spectra, total = pltpu.VMEM((seq, width), bf16), pltpu.VMEM((2 * seq, width), bf16), pltpu.VMEM((seq, width), f32)
    spec, *grad_inputs = call(
        functools.partial(input_body, parts),
        [rows(2 * seq, width, f32)] + [small] * parts,
        (gain, *taps, *grads, table),
        12 * seq * seq * width,
        (series, series, spectra, total),
    )
    grad_inputs = moved(grad_inputs, I)
    grad_filters = call(
        functools.partial(filter_body, parts),
        [small] * parts,
        (spec, *inputs, table),
        8 * seq * seq * width,
        (series, spectra, total),
    )
    grad_filters = moved(grad_filters, F)
    grad_input = call(functools.partial(join_body, I), [rows(span, channels)], grad_inputs, 0)[0]
    grad_filter = call(functools.partial(join_body, F), [rows(span, channels, f32)], grad_filters, 0)[0]
    return grad_input, grad_filter


def solution(mesh):
    return jax.shard_map(
        shards,
        mesh=mesh,
        in_specs=(
            P(("grp", "ctx"), "chan"),
            P(("grp", "ctx"), "chan"),
            P(("grp", "ctx"), "chan"),
            P("ctx", "chan"),
            P("chan"),
        ),
        out_specs=(P(("grp", "ctx"), "chan"), P(("grp", "ctx"), "chan")),
        check_vma=False,
    )
```
